1024 devices in a mesh: ctx: 128 (over x, y_lo, z), ch: 8 (over y_hi, core).
Axes of the slice: x: 8, y: 8 (y_hi: 4, y_lo: 2; y = y_hi * 2 + y_lo), z: 8, core: 2. Of those that a mesh axis runs over, the one named last changes fastest.
Arguments:
- query_act: bfloat16 [16384, 4096], P('ctx', 'ch'), may hold values from -6 to 6
- key_act: bfloat16 [16384, 4096], P('ctx', 'ch'), may hold values from -6 to 6
- value_act: bfloat16 [16384, 4096], P('ctx', 'ch'), may hold values from -6 to 6
- filters: bfloat16 [256, 128], P('ch'), may hold values from -0.5 to 0.5
- skip_bias: float32 [4096], P('ch'), may hold values from -4 to 4
- out_weight: bfloat16 [4096, 8192], P('ch'), may hold values from -0.09375 to 0.09375
- out_grad: bfloat16 [16384, 8192], P('ctx', 'ch'), may hold values from -6 to 6
Outputs:
- gated: bfloat16 [16384, 4096], P('ctx', 'ch')
- query_grad: bfloat16 [16384, 4096], P('ctx', 'ch')
- key_grad: bfloat16 [16384, 4096], P('ctx', 'ch')
- value_grad: bfloat16 [16384, 4096], P('ctx', 'ch')
- filter_grad: float32 [256, 128], P('ch')
- skip_grad: float32 [4096], P('ch')
The draws below stay inside these ranges and needn't reach their ends.
All inputs are finite; a program needn't handle non-finite values.
Results may differ from the reference program's by a relative error of at most 0.0075.
Values may be sent and summed in bfloat16 or wider, within the bound.
No kernel may reach another device: no remote copies, remote signals or barrier semaphores. Data moves between devices by JAX's collectives and lax.ppermute only.
A program may use at most 64 MiB of HBM per device.

```python
import jax
import jax.numpy as jnp
from jax import lax

C = 4096
DOUT = 8192
GSIZE = 16
TAPS = 128
TOKENS = 16384
GROUPS = 256


def level_of(own_key, shape, shards, low, top_value):
    level = 1.0
    for position, parts in shards:
        steps = jax.random.uniform(jax.random.fold_in(jax.random.fold_in(own_key, 6), position), (parts,), jnp.float32, low / len(shards), top_value / len(shards))
        level = level * jnp.repeat(jnp.exp(steps), shape[position] // parts).reshape((-1,) + (1,) * (len(shape) - 1 - position))
    return level


def bell_draw(rng, shape, spread, bound, split=(), kind=jnp.bfloat16):
    drawn = jax.random.normal(rng, shape, jnp.float32) * spread
    if len(split) > 0:
        drawn = level_of(rng, shape, split, -0.22, 0.18) * drawn
    return jnp.clip(drawn, min=-bound, max=bound).astype(kind)


def setup_inputs(seed: int = 0) -> dict:
    splits = jax.random.split(jax.random.key(seed), 8)
    query_act = bell_draw(splits[0], (TOKENS, C), 1.0, 6.0, ((0, 128), (1, 8)))
    key_act = bell_draw(splits[1], (TOKENS, C), 1.0, 6.0, ((0, 128), (1, 8)))
    value_act = bell_draw(splits[2], (TOKENS, C), 1.0, 6.0, ((0, 128), (1, 8)))
    filters = bell_draw(splits[3], (GROUPS, TAPS), TAPS ** -0.5, 0.5, ((0, 8),))
    skip_bias = bell_draw(splits[4], (C,), 1.0, 4.0, ((0, 8),), jnp.float32)
    out_weight = bell_draw(splits[5], (C, DOUT), C ** -0.5, 0.09375, ((0, 8),))
    out_grad = bell_draw(splits[6], (TOKENS, DOUT), 1.0, 6.0, ((0, 128), (1, 8)))
    return dict(query_act=query_act, key_act=key_act, value_act=value_act, filters=filters, skip_bias=skip_bias, out_weight=out_weight, out_grad=out_grad)


def filter_table(filt_blk, lag):
    valid = (lag >= 0) & (lag < TAPS)
    index_tab = jnp.clip(lag, 0, TAPS - 1)
    return jnp.where(valid[None], filt_blk[:, index_tab], jnp.zeros((), jnp.float32))


def reference(query_act, key_act, value_act, filters, skip_bias, out_weight, out_grad):
    blk = 256 if C % 256 == 0 else C
    nblk = C // blk
    gblk = blk // GSIZE
    nbt = TOKENS // TAPS
    rows_t = jnp.arange(TAPS, dtype=jnp.int32)[:, None]
    cols_s = jnp.arange(2 * TAPS - 1, dtype=jnp.int32)[None, :]
    fwd_lag = rows_t + (TAPS - 1) - cols_s
    bwd_lag = cols_s - rows_t
    taps_j = jnp.arange(TAPS, dtype=jnp.int32)[None, :]
    pick_idx = rows_t + (TAPS - 1) - taps_j

    def window_prev(series):
        blocks = series.reshape(nbt, TAPS, gblk, GSIZE)
        before = jnp.concatenate([jnp.zeros((1, TAPS, gblk, GSIZE), jnp.float32), blocks[:-1]], axis=0)
        return jnp.concatenate([before[:, 1:], blocks], axis=1)

    def window_next(series):
        blocks = series.reshape(nbt, TAPS, gblk, GSIZE)
        after = jnp.concatenate([blocks[1:], jnp.zeros((1, TAPS, gblk, GSIZE), jnp.float32)], axis=0)
        return jnp.concatenate([blocks, after[:, :TAPS - 1]], axis=1)

    def one_block(index):
        start = (index * blk).astype(jnp.int32)
        gstart = (index * gblk).astype(jnp.int32)
        query_f = lax.dynamic_slice_in_dim(query_act, start, blk, 1).astype(jnp.float32)
        key_f = lax.dynamic_slice_in_dim(key_act, start, blk, 1).astype(jnp.float32)
        value_f = lax.dynamic_slice_in_dim(value_act, start, blk, 1).astype(jnp.float32)
        filt = lax.dynamic_slice_in_dim(filters, gstart, gblk, 0).astype(jnp.float32)
        skip = lax.dynamic_slice_in_dim(skip_bias, start, blk, 0)
        weight_blk = lax.dynamic_slice_in_dim(out_weight, start, blk, 0)
        inner_f = (key_f * value_f).astype(jnp.bfloat16).astype(jnp.float32)
        inner_win = window_prev(inner_f)
        conv = jnp.einsum("gts,bsgc->btgc", filter_table(filt, fwd_lag), inner_win, precision=lax.Precision.HIGHEST).reshape(TOKENS, blk)
        mixed = conv + skip[None, :] * inner_f
        gated = (query_f * mixed).astype(jnp.bfloat16)
        mixed_grad = jnp.dot(out_grad, weight_blk.T, preferred_element_type=jnp.float32)
        query_grad = (mixed_grad * mixed).astype(jnp.bfloat16)
        conv_f = (mixed_grad * query_f).astype(jnp.bfloat16).astype(jnp.float32)
        grad_win = window_next(conv_f)
        back = jnp.einsum("gts,bsgc->btgc", filter_table(filt, bwd_lag), grad_win, precision=lax.Precision.HIGHEST).reshape(TOKENS, blk)
        inner_grad = back + skip[None, :] * conv_f
        key_grad = (inner_grad * value_f).astype(jnp.bfloat16)
        value_grad = (inner_grad * key_f).astype(jnp.bfloat16)
        pairs = jnp.einsum("btgc,bsgc->gts", conv_f.reshape(nbt, TAPS, gblk, GSIZE), inner_win, precision=lax.Precision.HIGHEST)
        picked = jnp.take_along_axis(pairs, jnp.broadcast_to(pick_idx[None], (gblk, TAPS, TAPS)), axis=2)
        filt_grad = jnp.sum(picked, axis=1)
        skip_grad = jnp.sum(conv_f * inner_f, axis=0)
        return gated, query_grad, key_grad, value_grad, filt_grad, skip_grad

    outs = lax.map(one_block, jnp.arange(nblk, dtype=jnp.int32))

    def joined(stack):
        return jnp.transpose(stack, (1, 0, 2)).reshape(TOKENS, C)

    return joined(outs[0]), joined(outs[1]), joined(outs[2]), joined(outs[3]), outs[4].reshape(GROUPS, TAPS), outs[5].reshape(C)
```

```python
import jax
import jax.numpy as jnp
from jax import lax
from jax.experimental import pallas as pl
from jax.experimental.pallas import tpu as pltpu
from jax.sharding import PartitionSpec as P


BF16 = jnp.bfloat16
F32 = jnp.float32
LANES = 128
Z_SIZE = 8
CORES = 2
SUM_ROWS = 40

VMEM_SPEC = pl.BlockSpec(memory_space=pltpu.VMEM)
SMEM_SPEC = pl.BlockSpec(memory_space=pltpu.SMEM)
NT = (((1,), (1,)), ((), ()))


def dot(a, b):
    return jnp.dot(a, b, preferred_element_type=F32)


def cost(flops, nbytes):
    return pl.CostEstimate(flops=flops, bytes_accessed=nbytes, transcendentals=0)


def group_mask(rows, group, group_size):
    lane = lax.broadcasted_iota(jnp.int32, (rows, LANES), 1)
    return (lane // group_size) == group


def reversal(size):
    row = lax.broadcasted_iota(jnp.int32, (size, size), 0)
    col = lax.broadcasted_iota(jnp.int32, (size, size), 1)
    return (row + col == size - 1).astype(BF16)


def grouped_conv(table_ref, series, group_size):
    tiles = []
    per_tile = LANES // group_size
    for tile in range(series.shape[1] // LANES):
        block = series[:, tile * LANES : (tile + 1) * LANES]
        total = None
        for g in range(per_tile):
            mask = group_mask(block.shape[0], g, group_size)
            part = jnp.where(mask, block, jnp.zeros_like(block))
            term = dot(table_ref[tile * per_tile + g], part)
            total = term if total is None else total + term
        tiles.append(total)
    return jnp.concatenate(tiles, axis=1)


def tables_kernel(filt_ref, fwd_ref, bwd_ref):
    groups, taps = filt_ref.shape
    filt = filt_ref[...]
    flipped = dot(filt, reversal(taps))
    filt = filt.astype(F32)
    zeros = jnp.zeros((1, taps), F32)
    for g in range(groups):
        for source, out_ref, first in ((flipped, fwd_ref, 1), (filt, bwd_ref, 0)):
            row = jnp.concatenate([source[g : g + 1], zeros], axis=1)
            full = jnp.broadcast_to(row, (taps, 2 * taps))
            out_ref[g] = pltpu.roll(
                full, first, axis=1, stride=1, stride_axis=0
            ).astype(BF16)


def forward_kernel(group_size, before_ref, inner_ref, query_ref, skip_ref, fwd_ref,
                   mixed_ref, gated_ref, flipped_ref):
    rows = inner_ref.shape[0]
    inner = inner_ref[...]
    series = jnp.concatenate([before_ref[...], inner], axis=0)
    mixed = grouped_conv(fwd_ref, series, group_size)
    mixed = mixed + skip_ref[...] * inner.astype(F32)
    mixed_ref[...] = mixed
    gated_ref[...] = (query_ref[...].astype(F32) * mixed).astype(BF16)
    flipped_ref[:rows - 16] = jnp.zeros((rows - 16, inner.shape[1]), BF16)
    flipped_ref[rows - 16 :] = dot(reversal(2 * rows), series).astype(BF16)


def partial_kernel(order_ref, first_ref, second_ref, weight_ref, acc_ref, out_ref):
    step = pl.program_id(0)

    @pl.when(step == 0)
    def _():
        out_ref[...] = acc_ref[...] + lax.dot_general(
            first_ref[...], weight_ref[...], NT, preferred_element_type=F32
        )

    @pl.when(step == 1)
    def _():
        out_ref[...] += lax.dot_general(
            second_ref[...], weight_ref[...], NT, preferred_element_type=F32
        )


def first_partial_kernel(order_ref, first_ref, second_ref, weight_ref, out_ref):
    step = pl.program_id(0)

    @pl.when(step == 0)
    def _():
        out_ref[...] = lax.dot_general(
            first_ref[...], weight_ref[...], NT, preferred_element_type=F32
        )

    @pl.when(step == 1)
    def _():
        out_ref[...] += lax.dot_general(
            second_ref[...], weight_ref[...], NT, preferred_element_type=F32
        )


def partial_product(order, first, second, weight, acc):
    rows, depth = first.shape
    width = weight.shape[0]
    whole = lambda shape: pl.BlockSpec(shape, lambda i, order: (0, 0))
    in_specs = [
        whole((rows, depth)),
        whole((rows, depth)),
        pl.BlockSpec((width, depth), lambda i, order: (0, order[i])),
    ]
    args = (order, first, second, weight)
    kernel = first_partial_kernel
    if acc is not None:
        in_specs.append(whole((rows, width)))
        args += (acc,)
        kernel = partial_kernel
    return pl.pallas_call(
        kernel,
        out_shape=jax.ShapeDtypeStruct((rows, width), F32),
        grid_spec=pltpu.PrefetchScalarGridSpec(
            num_scalar_prefetch=1,
            grid=(2,),
            in_specs=in_specs,
            out_specs=whole((rows, width)),
        ),
        compiler_params=pltpu.CompilerParams(vmem_limit_bytes=16 << 20),
        cost_estimate=cost(4 * rows * depth * width, 4 * width * depth),
        name="partial_product",
    )(*args)


def gradient_kernel(group_size, first_ref, second_ref, wfirst_ref, wsecond_ref, acc_ref,
                    query_ref, mixed_ref, inner_ref, flipped_ref,
                    conv_ref, qgrad_ref, sums_ref):
    rows, width = acc_ref.shape
    mixed_grad = (
        acc_ref[...]
        + lax.dot_general(first_ref[...], wfirst_ref[...], NT, preferred_element_type=F32)
        + lax.dot_general(second_ref[...], wsecond_ref[...], NT, preferred_element_type=F32)
    )
    conv = (mixed_grad * query_ref[...].astype(F32)).astype(BF16)
    conv_ref[...] = conv
    qgrad_ref[...] = (mixed_grad * mixed_ref[...]).astype(BF16)
    skip = jnp.sum(conv.astype(F32) * inner_ref[...].astype(F32), axis=0, keepdims=True)
    per_tile = LANES // group_size
    span = 2 * rows
    sub = 16
    row_group = lax.broadcasted_iota(jnp.int32, (per_tile * sub, LANES), 0) // sub
    lane_group = lax.broadcasted_iota(jnp.int32, (per_tile * sub, LANES), 1) // group_size
    own = row_group == lane_group
    for tile in range(width // LANES):
        lanes = slice(tile * LANES, (tile + 1) * LANES)
        total = None
        for a in range(rows // sub):
            part = conv[a * sub : (a + 1) * sub, lanes]
            spread = jnp.concatenate([part] * per_tile, axis=0)
            spread = jnp.where(own, spread, jnp.zeros_like(spread))
            start = rows - sub - a * sub
            term = lax.dot_general(
                spread, flipped_ref[start : start + span, lanes], NT,
                preferred_element_type=F32,
            )
            total = term if total is None else total + term
        for g in range(per_tile):
            skewed = pltpu.roll(
                total[g * sub : (g + 1) * sub], 1, axis=1, stride=1, stride_axis=0
            )
            row = tile * per_tile + g
            sums_ref[row : row + 1] = jnp.sum(skewed[:, rows:], axis=0, keepdims=True)
        row = width // group_size + tile
        sums_ref[row : row + 1] = skip[:, lanes]
    used = width // group_size + width // LANES
    sums_ref[used:] = jnp.zeros((sums_ref.shape[0] - used, LANES), F32)


def backward_kernel(group_size, conv_ref, after_ref, key_ref, value_ref, skip_ref, bwd_ref,
                    kgrad_ref, vgrad_ref):
    conv = conv_ref[...]
    series = jnp.concatenate([conv, after_ref[...]], axis=0)
    grad = grouped_conv(bwd_ref, series, group_size)
    grad = grad + skip_ref[...] * conv.astype(F32)
    kgrad_ref[...] = (grad * value_ref[...].astype(F32)).astype(BF16)
    vgrad_ref[...] = (grad * key_ref[...].astype(F32)).astype(BF16)


def call(kernel, outs, args, name, flops, nbytes):
    return pl.pallas_call(
        kernel,
        out_shape=[jax.ShapeDtypeStruct(s, d) for s, d in outs],
        in_specs=[VMEM_SPEC] * len(args),
        out_specs=[VMEM_SPEC] * len(outs),
        compiler_params=pltpu.CompilerParams(vmem_limit_bytes=24 << 20),
        cost_estimate=cost(flops, nbytes),
        name=name,
    )(*args)


def passed_along(block, axis, distance):
    devices = range(lax.axis_size(axis))
    route = [(i - distance, i) for i in devices if i - distance in devices]
    return lax.ppermute(block, axis, route)


def summed_over(block, axis, groups):
    count = len(groups[0])
    spread = jnp.broadcast_to(block[None], (count,) + block.shape)
    got = lax.all_to_all(spread, axis, 0, 0, axis_index_groups=groups, tiled=True)
    return jnp.sum(got, axis=0)


def per_device(query_act, key_act, value_act, filters, skip_bias, out_weight, out_grad):
    rows, width = query_act.shape
    groups, taps = filters.shape
    group_size = width // groups
    depth = out_grad.shape[1]
    ch_size = lax.axis_size("ch")
    ctx_size = lax.axis_size("ctx")
    chips = ch_size // CORES

    def ring(block):
        to = lambda c: ((c // CORES + (1 if c % CORES == 0 else -1)) % chips) * CORES + c % CORES
        return lax.ppermute(block, "ch", [(c, to(c)) for c in range(ch_size)])

    def swap(block):
        return lax.ppermute(block, "ch", [(c, c ^ 1) for c in range(ch_size)])

    me = lax.axis_index("ch")
    chip, core = me // CORES, me % CORES
    step = 1 - 2 * core
    at = lambda c, k: (lax.rem(c + 2 * chips, chips) * CORES + k).astype(jnp.int32)

    skip_row = skip_bias.reshape(1, width)
    inner = (key_act.astype(F32) * value_act.astype(F32)).astype(BF16)

    ring1 = ring(out_grad)
    swap0 = swap(out_grad)
    before = passed_along(inner, "ctx", 1)
    ring2 = ring(swap0)
    fwd, bwd = call(
        tables_kernel,
        [((groups, taps, 2 * taps), BF16)] * 2,
        (filters,),
        "tables",
        8 * groups * taps * taps,
        8 * groups * taps * taps,
    )
    ring3 = ring(ring1)
    swap1 = swap(ring1)
    mixed, gated, flipped = call(
        lambda *refs: forward_kernel(group_size, *refs),
        [((rows, width), F32), ((rows, width), BF16), ((3 * rows - 16, width), BF16)],
        (before, inner, query_act, skip_row, fwd),
        "forward",
        4 * rows * rows * width * 8,
        4 << 20,
    )
    swap2 = swap(ring2)
    swap3 = swap(ring3)

    acc = partial_product(
        jnp.stack([at(chip, core), at(chip, 1 - core)]), out_grad, swap0, out_weight, None
    )
    acc = partial_product(
        jnp.stack([at(chip - step, core), at(chip + step, 1 - core)]),
        ring1, swap1, out_weight, acc,
    )
    acc = partial_product(
        jnp.stack([at(chip - step, 1 - core), at(chip + step, core)]),
        ring2, swap2, out_weight, acc,
    )
    w_last = [
        lax.dynamic_slice(out_weight, (0, at(chip + 2, k) * depth), (width, depth))
        for k in (core, 1 - core)
    ]
    conv, query_grad, sums = call(
        lambda *refs: gradient_kernel(group_size, *refs),
        [((rows, width), BF16), ((rows, width), BF16), ((SUM_ROWS, LANES), F32)],
        (ring3, swap3, w_last[0], w_last[1], acc, query_act, mixed, inner, flipped),
        "gradient",
        8 * rows * depth * width,
        4 << 20,
    )
    after = passed_along(conv, "ctx", -1)
    planes = ctx_size // Z_SIZE
    along_z = [[p * Z_SIZE + z for z in range(Z_SIZE)] for p in range(planes)]
    across_z = [[p * Z_SIZE + z for p in range(planes)] for z in range(Z_SIZE)]
    sums = summed_over(sums, "ctx", along_z)
    sums = summed_over(sums, "ctx", across_z)
    key_grad, value_grad = call(
        lambda *refs: backward_kernel(group_size, *refs),
        [((rows, width), BF16)] * 2,
        (conv, after, key_act, value_act, skip_row, bwd),
        "backward",
        4 * rows * rows * width * 8,
        4 << 20,
    )
    filter_grad = sums[:groups]
    skip_grad = sums[groups : groups + width // LANES].reshape(width)
    return gated, query_grad, key_grad, value_grad, filter_grad, skip_grad


def solution(mesh):
    wide, narrow = P("ctx", "ch"), P("ch", None)
    return jax.shard_map(
        per_device,
        mesh=mesh,
        in_specs=(wide, wide, wide, narrow, P("ch"), narrow, wide),
        out_specs=(wide, wide, wide, wide, narrow, P("ch")),
        check_vma=False,
    )
```

```python
import functools

import jax
import jax.numpy as jnp
from jax import lax
from jax.experimental import pallas as pl
from jax.experimental.pallas import tpu as pltpu
from jax.sharding import PartitionSpec as P


BF16 = jnp.bfloat16
F32 = jnp.float32
LANES = 128
Z_SIZE = 8
CORES = 2

VMEM_SPEC = pl.BlockSpec(memory_space=pltpu.VMEM)
SMEM_SPEC = pl.BlockSpec(memory_space=pltpu.SMEM)
NT = (((1,), (1,)), ((), ()))


def dot(a, b):
    return jnp.dot(a, b, preferred_element_type=F32)


def cost(flops, nbytes):
    return pl.CostEstimate(flops=flops, bytes_accessed=nbytes, transcendentals=0)


def group_mask(rows, group, group_size):
    lane = lax.broadcasted_iota(jnp.int32, (rows, LANES), 1)
    return (lane // group_size) == group


def reversal(size):
    row = lax.broadcasted_iota(jnp.int32, (size, size), 0)
    col = lax.broadcasted_iota(jnp.int32, (size, size), 1)
    return (row + col == size - 1).astype(BF16)


def grouped_conv(table_ref, series, group_size):
    tiles = []
    per_tile = LANES // group_size
    for tile in range(series.shape[1] // LANES):
        block = series[:, tile * LANES : (tile + 1) * LANES]
        total = None
        for g in range(per_tile):
            mask = group_mask(block.shape[0], g, group_size)
            part = jnp.where(mask, block, jnp.zeros_like(block))
            term = dot(table_ref[tile * per_tile + g], part)
            total = term if total is None else total + term
        tiles.append(total)
    return jnp.concatenate(tiles, axis=1)


def stage_kernel(filt_ref, weight_hbm, fwd_ref, bwd_ref, weight_ref, sem):
    pieces = sem.shape[0]
    height = weight_hbm.shape[0] // pieces
    copies = []
    for i in range(pieces):
        rows = pl.ds(i * height, height)
        copies.append(
            pltpu.make_async_copy(weight_hbm.at[rows], weight_ref.at[rows], sem.at[i])
        )
        copies[-1].start()
    groups, taps = filt_ref.shape
    filt = filt_ref[...]
    flipped = dot(filt, reversal(taps))
    filt = filt.astype(F32)
    zeros = jnp.zeros((1, taps), F32)
    for g in range(groups):
        for source, out_ref, first in ((flipped, fwd_ref, 1), (filt, bwd_ref, 0)):
            row = jnp.concatenate([source[g : g + 1], zeros], axis=1)
            full = jnp.broadcast_to(row, (taps, 2 * taps))
            out_ref[g] = pltpu.roll(
                full, first, axis=1, stride=1, stride_axis=0
            ).astype(BF16)
    for copy in copies:
        copy.wait()


def forward_kernel(group_size, before_ref, inner_ref, query_ref, skip_ref, fwd_ref,
                   mixed_ref, gated_ref, flipped_ref):
    rows = inner_ref.shape[0]
    inner = inner_ref[...]
    series = jnp.concatenate([before_ref[...], inner], axis=0)
    mixed = grouped_conv(fwd_ref, series, group_size)
    mixed = mixed + skip_ref[...] * inner.astype(F32)
    mixed_ref[...] = mixed
    gated_ref[...] = (query_ref[...].astype(F32) * mixed).astype(BF16)
    flipped_ref[:rows - 16] = jnp.zeros((rows - 16, inner.shape[1]), BF16)
    flipped_ref[rows - 16 :] = dot(reversal(2 * rows), series).astype(BF16)


def product(block, weight_ref, position):
    depth = block.shape[1]
    columns = pl.ds(pl.multiple_of(position * depth, depth), depth)
    return lax.dot_general(block, weight_ref[:, columns], NT, preferred_element_type=F32)


def partial_kernel(start, order_ref, weight_ref, *refs):
    blocks, acc_ref, out_ref = refs[:2], refs[2:-1], refs[-1]
    total = acc_ref[0][...] if acc_ref else None
    for i, block_ref in enumerate(blocks):
        term = product(block_ref[...], weight_ref, order_ref[start + i])
        total = term if total is None else total + term
    out_ref[...] = total


def gradient_kernel(group_size, start, order_ref, weight_ref, first_ref, second_ref, acc_ref,
                    query_ref, mixed_ref, inner_ref, flipped_ref,
                    conv_ref, qgrad_ref, sums_ref):
    rows, width = acc_ref.shape
    mixed_grad = (
        acc_ref[...]
        + product(first_ref[...], weight_ref, order_ref[start])
        + product(second_ref[...], weight_ref, order_ref[start + 1])
    )
    conv = (mixed_grad * query_ref[...].astype(F32)).astype(BF16)
    conv_ref[...] = conv
    qgrad_ref[...] = (mixed_grad * mixed_ref[...]).astype(BF16)
    skip = jnp.sum(conv.astype(F32) * inner_ref[...].astype(F32), axis=0, keepdims=True)
    per_tile = LANES // group_size
    span = 2 * rows
    sub = 16
    row_group = lax.broadcasted_iota(jnp.int32, (per_tile * sub, LANES), 0) // sub
    lane_group = lax.broadcasted_iota(jnp.int32, (per_tile * sub, LANES), 1) // group_size
    own = row_group == lane_group
    for tile in range(width // LANES):
        lanes = slice(tile * LANES, (tile + 1) * LANES)
        total = None
        for a in range(rows // sub):
            part = conv[a * sub : (a + 1) * sub, lanes]
            spread = jnp.concatenate([part] * per_tile, axis=0)
            spread = jnp.where(own, spread, jnp.zeros_like(spread))
            start = rows - sub - a * sub
            term = lax.dot_general(
                spread, flipped_ref[start : start + span, lanes], NT,
                preferred_element_type=F32,
            )
            total = term if total is None else total + term
        for g in range(per_tile):
            skewed = pltpu.roll(
                total[g * sub : (g + 1) * sub], 1, axis=1, stride=1, stride_axis=0
            )
            row = tile * per_tile + g
            sums_ref[row : row + 1] = jnp.sum(skewed[:, rows:], axis=0, keepdims=True)
        row = width // group_size + tile
        sums_ref[row : row + 1] = skip[:, lanes]
    used = width // group_size + width // LANES
    sums_ref[used:] = jnp.zeros((sums_ref.shape[0] - used, LANES), F32)


def backward_kernel(group_size, conv_ref, after_ref, key_ref, value_ref, skip_ref, bwd_ref,
                    kgrad_ref, vgrad_ref):
    conv = conv_ref[...]
    series = jnp.concatenate([conv, after_ref[...]], axis=0)
    grad = grouped_conv(bwd_ref, series, group_size)
    grad = grad + skip_ref[...] * conv.astype(F32)
    kgrad_ref[...] = (grad * value_ref[...].astype(F32)).astype(BF16)
    vgrad_ref[...] = (grad * key_ref[...].astype(F32)).astype(BF16)


def call(kernel, outs, args, flops, specs=None, scratch=(), vmem=24):
    return pl.pallas_call(
        kernel,
        out_shape=[jax.ShapeDtypeStruct(s, d) for s, d in outs],
        in_specs=specs or [VMEM_SPEC] * len(args),
        out_specs=[VMEM_SPEC] * len(outs),
        scratch_shapes=scratch,
        compiler_params=pltpu.CompilerParams(vmem_limit_bytes=vmem << 20),
        cost_estimate=cost(flops, 4 << 20),
    )(*args)


def passed_along(block, axis, distance):
    devices = range(lax.axis_size(axis))
    route = [(i - distance, i) for i in devices if i - distance in devices]
    return lax.ppermute(block, axis, route)


def exchanged(blocks, groups):
    return lax.all_to_all(blocks, "ctx", 0, 0, axis_index_groups=groups, tiled=True)


def spread(block, count):
    return jnp.broadcast_to(block[None], (count,) + block.shape)


def per_device(query_act, key_act, value_act, filters, skip_bias, out_weight, out_grad):
    rows, width = query_act.shape
    groups, taps = filters.shape
    group_size = width // groups
    depth = out_grad.shape[1]
    ch_size = lax.axis_size("ch")
    ctx_size = lax.axis_size("ctx")
    chips = ch_size // CORES

    def ring(block):
        to = lambda c: ((c // CORES + (1 if c % CORES == 0 else -1)) % chips) * CORES + c % CORES
        return lax.ppermute(block, "ch", [(c, to(c)) for c in range(ch_size)])

    def swap(block):
        return lax.ppermute(block, "ch", [(c, c ^ 1) for c in range(ch_size)])

    me = lax.axis_index("ch")
    chip, core = me // CORES, me % CORES
    ahead = jnp.array([0, 0, -1, 1, -1, 1, 2, 2], jnp.int32) * (1 - 2 * core)
    other = jnp.array([0, 1, 0, 1, 1, 0, 0, 1], jnp.int32)
    order = (((chip + ahead) % chips) * CORES + (core ^ other)).astype(jnp.int32)

    skip_row = skip_bias.reshape(1, width)
    inner = (key_act.astype(F32) * value_act.astype(F32)).astype(BF16)

    ring1 = ring(out_grad)
    swap0 = swap(out_grad)
    before = passed_along(inner, "ctx", 1)
    ring2 = ring(swap0)
    fwd, bwd, weight = call(
        stage_kernel,
        [((groups, taps, 2 * taps), BF16)] * 2 + [(out_weight.shape, BF16)],
        (filters, out_weight),
        8 * groups * taps * taps,
        [VMEM_SPEC, pl.BlockSpec(memory_space=pltpu.HBM)],
        [pltpu.SemaphoreType.DMA((8,))],
        40,
    )
    ring3 = ring(ring1)
    swap1 = swap(ring1)
    mixed, gated, flipped = call(
        lambda *refs: forward_kernel(group_size, *refs),
        [((rows, width), F32), ((rows, width), BF16), ((3 * rows - 16, width), BF16)],
        (before, inner, query_act, skip_row, fwd),
        4 * rows * rows * width * 8,
    )
    swap2 = swap(ring2)
    swap3 = swap(ring3)

    acc = ()
    for i, pair in enumerate(((out_grad, swap0), (ring1, swap1), (ring2, swap2))):
        acc = call(
            functools.partial(partial_kernel, 2 * i),
            [((rows, width), F32)],
            (order, weight, *pair, *acc),
            4 * rows * depth * width,
            [SMEM_SPEC] + [VMEM_SPEC] * (3 + len(acc)),
        )
    conv, query_grad, sums = call(
        functools.partial(gradient_kernel, group_size, 6),
        [((rows, width), BF16), ((rows, width), BF16), ((Z_SIZE * 8, LANES), F32)],
        (order, weight, ring3, swap3, *acc, query_act, mixed, inner, flipped),
        8 * rows * depth * width,
        [SMEM_SPEC] + [VMEM_SPEC] * 8,
    )
    planes = ctx_size // Z_SIZE
    along_z = [[p * Z_SIZE + z for z in range(Z_SIZE)] for p in range(planes)]
    across_z = [[p * Z_SIZE + z for p in range(planes)] for z in range(Z_SIZE)]
    sums = jnp.sum(exchanged(sums.reshape(Z_SIZE, 8, LANES), along_z), axis=0)
    after = passed_along(conv, "ctx", -1)
    sums = jnp.sum(exchanged(spread(sums, planes), across_z), axis=0)
    sums = exchanged(spread(sums, Z_SIZE), along_z).reshape(Z_SIZE * 8, LANES)
    key_grad, value_grad = call(
        lambda *refs: backward_kernel(group_size, *refs),
        [((rows, width), BF16)] * 2,
        (conv, after, key_act, value_act, skip_row, bwd),
        4 * rows * rows * width * 8,
    )
    filter_grad = sums[:groups]
    skip_grad = sums[groups : groups + width // LANES].reshape(width)
    return gated, query_grad, key_grad, value_grad, filter_grad, skip_grad


def solution(mesh):
    wide, narrow = P("ctx", "ch"), P("ch", None)

    return jax.shard_map(
        per_device,
        mesh=mesh,
        in_specs=(wide, wide, wide, narrow, P("ch"), narrow, wide),
        out_specs=(wide, wide, wide, wide, narrow, P("ch")),
        check_vma=False,
    )
```

```python
import functools

import jax
import jax.numpy as jnp
from jax import lax
from jax.experimental import pallas as pl
from jax.experimental.pallas import tpu as pltpu
from jax.sharding import PartitionSpec as P


BF16 = jnp.bfloat16
F32 = jnp.float32
LANES = 128
Z_SIZE = 8
CORES = 2
SUM_ROWS = 40
VMEM_MIB = 44
PAIR_DISTANCE = (0, -1, 1, 2)
SWAPPED_PAIR = 2

VMEM_SPEC = pl.BlockSpec(memory_space=pltpu.VMEM)
NT = (((1,), (1,)), ((), ()))


def dot(a, b):
    return jnp.dot(a, b, preferred_element_type=F32)


def cost(flops, nbytes):
    return pl.CostEstimate(flops=flops, bytes_accessed=nbytes, transcendentals=0)


def group_mask(rows, group, group_size):
    lane = lax.broadcasted_iota(jnp.int32, (rows, LANES), 1)
    return (lane // group_size) == group


def reversal(size):
    row = lax.broadcasted_iota(jnp.int32, (size, size), 0)
    col = lax.broadcasted_iota(jnp.int32, (size, size), 1)
    return (row + col == size - 1).astype(BF16)


def grouped_conv(table_ref, series, group_size):
    tiles = []
    per_tile = LANES // group_size
    for tile in range(series.shape[1] // LANES):
        block = series[:, tile * LANES : (tile + 1) * LANES]
        total = None
        for g in range(per_tile):
            mask = group_mask(block.shape[0], g, group_size)
            part = jnp.where(mask, block, jnp.zeros_like(block))
            term = dot(table_ref[tile * per_tile + g], part)
            total = term if total is None else total + term
        tiles.append(total)
    return jnp.concatenate(tiles, axis=1)


def positions(pair):
    size = lax.axis_size("ch")
    me = lax.axis_index("ch")
    chips = size // CORES
    chip, core = me // CORES, me % CORES
    step = 1 - 2 * core
    owner = (chip + PAIR_DISTANCE[pair] * step + chips) % chips
    first = 1 - core if pair == SWAPPED_PAIR else core
    return [owner * CORES + first, owner * CORES + 1 - first]


def fetched(weight_hbm, pair_ref, sem, pair):
    depth = pair_ref.shape[2]
    copies = []
    for i, position in enumerate(positions(pair)):
        columns = pl.ds(pl.multiple_of(position * depth, depth), depth)
        copies.append(
            pltpu.make_async_copy(weight_hbm.at[:, columns], pair_ref.at[i], sem.at[i])
        )
        copies[-1].start()
    return copies


def finished(copies):
    for copy in copies:
        copy.wait()


def stage_kernel(filt_ref, weight_hbm, fwd_ref, bwd_ref, pair_ref, sem):
    copies = fetched(weight_hbm, pair_ref, sem, 0)
    groups, taps = filt_ref.shape
    filt = filt_ref[...]
    flipped = dot(filt, reversal(taps))
    filt = filt.astype(F32)
    zeros = jnp.zeros((1, taps), F32)
    for g in range(groups):
        for source, out_ref, first in ((flipped, fwd_ref, 1), (filt, bwd_ref, 0)):
            row = jnp.concatenate([source[g : g + 1], zeros], axis=1)
            full = jnp.broadcast_to(row, (taps, 2 * taps))
            out_ref[g] = pltpu.roll(
                full, first, axis=1, stride=1, stride_axis=0
            ).astype(BF16)
    finished(copies)


def forward_kernel(group_size, before_ref, inner_ref, query_ref, skip_ref, fwd_ref,
                   ring1_ref, ring2_ref, weight_hbm,
                   mixed_ref, gated_ref, flipped_ref, packed_ref, pair_ref, sem):
    copies = fetched(weight_hbm, pair_ref, sem, 2)
    packed_ref[0] = ring1_ref[...]
    packed_ref[1] = ring2_ref[...]
    rows = inner_ref.shape[0]
    inner = inner_ref[...]
    series = jnp.concatenate([before_ref[...], inner], axis=0)
    mixed = grouped_conv(fwd_ref, series, group_size)
    mixed = mixed + skip_ref[...] * inner.astype(F32)
    mixed_ref[...] = mixed
    gated_ref[...] = (query_ref[...].astype(F32) * mixed).astype(BF16)
    flipped_ref[:rows - 16] = jnp.zeros((rows - 16, inner.shape[1]), BF16)
    flipped_ref[rows - 16 :] = dot(reversal(2 * rows), series).astype(BF16)
    finished(copies)


def products(blocks, pair_ref):
    total = None
    for i, block in enumerate(blocks):
        term = lax.dot_general(block, pair_ref[i], NT, preferred_element_type=F32)
        total = term if total is None else total + term
    return total


def first_product_kernel(own_ref, swap_ref, pair_ref, weight_hbm, out_ref, next_ref, sem):
    copies = fetched(weight_hbm, next_ref, sem, 1)
    out_ref[...] = products((own_ref[...], swap_ref[...]), pair_ref)
    finished(copies)


def second_product_kernel(ring1_ref, ring2_ref, pair_ref, acc_ref, weight_hbm,
                          out_ref, next_ref, sem):
    copies = fetched(weight_hbm, next_ref, sem, 3)
    out_ref[...] = acc_ref[...] + products((ring1_ref[...], ring2_ref[...]), pair_ref)
    finished(copies)


def third_product_kernel(swaps_ref, pair_ref, acc_ref, out_ref):
    out_ref[...] = acc_ref[...] + products((swaps_ref[0], swaps_ref[1]), pair_ref)


def gradient_kernel(group_size, pair_ref, first_ref, second_ref, acc_ref,
                    query_ref, mixed_ref, inner_ref, flipped_ref,
                    conv_ref, qgrad_ref, sums_ref):
    rows, width = acc_ref.shape
    mixed_grad = acc_ref[...] + products((first_ref[...], second_ref[...]), pair_ref)
    conv = (mixed_grad * query_ref[...].astype(F32)).astype(BF16)
    conv_ref[...] = conv
    qgrad_ref[...] = (mixed_grad * mixed_ref[...]).astype(BF16)
    skip = jnp.sum(conv.astype(F32) * inner_ref[...].astype(F32), axis=0, keepdims=True)
    per_tile = LANES // group_size
    span = 2 * rows
    sub = 16
    row_group = lax.broadcasted_iota(jnp.int32, (per_tile * sub, LANES), 0) // sub
    lane_group = lax.broadcasted_iota(jnp.int32, (per_tile * sub, LANES), 1) // group_size
    own = row_group == lane_group
    found = []
    for tile in range(width // LANES):
        lanes = slice(tile * LANES, (tile + 1) * LANES)
        total = None
        for a in range(rows // sub):
            part = conv[a * sub : (a + 1) * sub, lanes]
            spread = jnp.concatenate([part] * per_tile, axis=0)
            spread = jnp.where(own, spread, jnp.zeros_like(spread))
            start = rows - sub - a * sub
            term = lax.dot_general(
                spread, flipped_ref[start : start + span, lanes], NT,
                preferred_element_type=F32,
            )
            total = term if total is None else total + term
        for g in range(per_tile):
            skewed = pltpu.roll(
                total[g * sub : (g + 1) * sub], 1, axis=1, stride=1, stride_axis=0
            )
            found.append(jnp.sum(skewed[:, rows:], axis=0, keepdims=True))
    found += [skip[:, i * LANES : (i + 1) * LANES] for i in range(width // LANES)]
    found.append(jnp.zeros((sums_ref.shape[1] - len(found), LANES), F32))
    sums = jnp.concatenate(found, axis=0)
    for i in range(sums_ref.shape[0]):
        sums_ref[i] = sums


def fold_kernel(got_ref, out_ref):
    total = jnp.sum(got_ref[...], axis=0)
    for i in range(out_ref.shape[0]):
        out_ref[i] = total


def finish_kernel(got_ref, filter_ref, skip_ref):
    total = jnp.sum(got_ref[...], axis=0)
    groups = filter_ref.shape[0]
    filter_ref[...] = total[:groups]
    for i in range(skip_ref.shape[1] // LANES):
        skip_ref[:, i * LANES : (i + 1) * LANES] = total[groups + i : groups + i + 1]


def backward_kernel(group_size, conv_ref, after_ref, key_ref, value_ref, skip_ref, bwd_ref,
                    kgrad_ref, vgrad_ref):
    conv = conv_ref[...]
    series = jnp.concatenate([conv, after_ref[...]], axis=0)
    grad = grouped_conv(bwd_ref, series, group_size)
    grad = grad + skip_ref[...] * conv.astype(F32)
    kgrad_ref[...] = (grad * value_ref[...].astype(F32)).astype(BF16)
    vgrad_ref[...] = (grad * key_ref[...].astype(F32)).astype(BF16)


def call(kernel, outs, args, flops, specs=None, scratch=(), vmem=24):
    return pl.pallas_call(
        kernel,
        out_shape=[jax.ShapeDtypeStruct(s, d) for s, d in outs],
        in_specs=specs or [VMEM_SPEC] * len(args),
        out_specs=[VMEM_SPEC] * len(outs),
        scratch_shapes=scratch,
        compiler_params=pltpu.CompilerParams(vmem_limit_bytes=vmem << 20),
        cost_estimate=cost(flops, 4 << 20),
    )(*args)


def passed_along(block, axis, distance):
    devices = range(lax.axis_size(axis))
    route = [(i - distance, i) for i in devices if i - distance in devices]
    return lax.ppermute(block, axis, route)


def exchanged(blocks, groups):
    return lax.all_to_all(blocks, "ctx", 0, 0, axis_index_groups=groups, tiled=True)


def per_device(query_act, key_act, value_act, filters, skip_bias, out_weight, out_grad):
    rows, width = query_act.shape
    groups, taps = filters.shape
    group_size = width // groups
    depth = out_grad.shape[1]
    ch_size = lax.axis_size("ch")
    ctx_size = lax.axis_size("ctx")
    chips = ch_size // CORES

    def ring(block):
        to = lambda c: ((c // CORES + (1 if c % CORES == 0 else -1)) % chips) * CORES + c % CORES
        return lax.ppermute(block, "ch", [(c, to(c)) for c in range(ch_size)])

    def swap(block):
        return lax.ppermute(block, "ch", [(c, c ^ 1) for c in range(ch_size)])

    skip_row = skip_bias.reshape(1, width)
    inner = (key_act.astype(F32) * value_act.astype(F32)).astype(BF16)

    hbm = pl.BlockSpec(memory_space=pltpu.HBM)
    pair = ((2, width, depth), BF16)
    wide = (rows, width)
    sem = [pltpu.SemaphoreType.DMA((2,))]

    ring1 = ring(out_grad)
    swap0 = swap(out_grad)
    before = passed_along(inner, "ctx", 1)
    ring2 = ring(swap0)
    fwd, bwd, pair0 = call(
        stage_kernel,
        [((groups, taps, 2 * taps), BF16)] * 2 + [pair],
        (filters, out_weight),
        8 * groups * taps * taps,
        [VMEM_SPEC, hbm],
        sem,
        VMEM_MIB,
    )
    acc, pair1 = call(
        first_product_kernel,
        [(wide, F32), pair],
        (out_grad, swap0, pair0, out_weight),
        4 * rows * depth * width,
        [VMEM_SPEC] * 3 + [hbm],
        sem,
        VMEM_MIB,
    )
    ring3 = ring(ring1)
    mixed, gated, flipped, packed, pair2 = call(
        functools.partial(forward_kernel, group_size),
        [(wide, F32), (wide, BF16), ((3 * rows - 16, width), BF16), ((2, rows, depth), BF16), pair],
        (before, inner, query_act, skip_row, fwd, ring1, ring2, out_weight),
        4 * rows * rows * width * 8,
        [VMEM_SPEC] * 7 + [hbm],
        sem,
        VMEM_MIB,
    )
    swap12 = swap(packed)
    acc, pair3 = call(
        second_product_kernel,
        [(wide, F32), pair],
        (ring1, ring2, pair1, acc, out_weight),
        4 * rows * depth * width,
        [VMEM_SPEC] * 4 + [hbm],
        sem,
        VMEM_MIB,
    )
    swap3 = swap(ring3)
    acc = call(
        third_product_kernel, [(wide, F32)], (swap12, pair2, acc), 4 * rows * depth * width
    )[0]
    planes = ctx_size // Z_SIZE
    conv, query_grad, sums = call(
        functools.partial(gradient_kernel, group_size),
        [(wide, BF16), (wide, BF16), ((Z_SIZE, SUM_ROWS, LANES), F32)],
        (pair3, ring3, swap3, acc, query_act, mixed, inner, flipped),
        8 * rows * depth * width,
    )
    along_z = [[p * Z_SIZE + z for z in range(Z_SIZE)] for p in range(planes)]
    across_z = [[p * Z_SIZE + z for p in range(planes)] for z in range(Z_SIZE)]
    sums = exchanged(sums, along_z)
    after = passed_along(conv, "ctx", -1)
    sums = call(fold_kernel, [((planes, SUM_ROWS, LANES), F32)], (sums,), 1 << 20)[0]
    sums = exchanged(sums, across_z)
    key_grad, value_grad = call(
        functools.partial(backward_kernel, group_size),
        [(wide, BF16)] * 2,
        (conv, after, key_act, value_act, skip_row, bwd),
        4 * rows * rows * width * 8,
    )
    filter_grad, skip_grad = call(
        finish_kernel, [((groups, LANES), F32), ((1, width), F32)], (sums,), 1 << 20
    )
    return gated, query_grad, key_grad, value_grad, filter_grad, skip_grad.reshape(width)


def solution(mesh):
    wide, narrow = P("ctx", "ch"), P("ch", None)

    return jax.shard_map(
        per_device,
        mesh=mesh,
        in_specs=(wide, wide, wide, narrow, P("ch"), narrow, wide),
        out_specs=(wide, wide, wide, wide, narrow, P("ch")),
        check_vma=False,
    )
```

```python
import functools

import jax
import jax.numpy as jnp
from jax import lax
from jax.experimental import pallas as pl
from jax.experimental.pallas import tpu as pltpu
from jax.sharding import PartitionSpec as P


BF16 = jnp.bfloat16
F32 = jnp.float32
LANES = 128
Z_SIZE = 8
CORES = 2
SUM_ROWS = 40
PIECES = 4
VMEM_MIB = 42
PAIR_DISTANCE = (0, -1, 1, 2)
SWAPPED_PAIR = 2

VMEM_SPEC = pl.BlockSpec(memory_space=pltpu.VMEM)
NT = (((1,), (1,)), ((), ()))


def dot(a, b):
    return jnp.dot(a, b, preferred_element_type=F32)


def cost(flops, nbytes):
    return pl.CostEstimate(flops=flops, bytes_accessed=nbytes, transcendentals=0)


def group_mask(rows, group, group_size):
    lane = lax.broadcasted_iota(jnp.int32, (rows, LANES), 1)
    return (lane // group_size) == group


def reversal(size):
    row = lax.broadcasted_iota(jnp.int32, (size, size), 0)
    col = lax.broadcasted_iota(jnp.int32, (size, size), 1)
    return (row + col == size - 1).astype(BF16)


def grouped_conv(table_ref, series, group_size):
    tiles = []
    per_tile = LANES // group_size
    for tile in range(series.shape[1] // LANES):
        block = series[:, tile * LANES : (tile + 1) * LANES]
        total = None
        for g in range(per_tile):
            mask = group_mask(block.shape[0], g, group_size)
            part = jnp.where(mask, block, jnp.zeros_like(block))
            term = dot(table_ref[tile * per_tile + g], part)
            total = term if total is None else total + term
        tiles.append(total)
    return jnp.concatenate(tiles, axis=1)


def positions(pair):
    size = lax.axis_size("ch")
    me = lax.axis_index("ch")
    chips = size // CORES
    chip, core = me // CORES, me % CORES
    step = 1 - 2 * core
    owner = (chip + PAIR_DISTANCE[pair] * step + chips) % chips
    first = 1 - core if pair == SWAPPED_PAIR else core
    return [owner * CORES + first, owner * CORES + 1 - first]


def fetched(weight_hbm, pair_ref, sem, pair):
    depth = pair_ref.shape[2]
    height = pair_ref.shape[1] // PIECES
    copies = []
    for i, position in enumerate(positions(pair)):
        columns = pl.ds(pl.multiple_of(position * depth, depth), depth)
        for j in range(PIECES):
            rows = pl.ds(j * height, height)
            source, target = weight_hbm.at[rows, columns], pair_ref.at[i, rows]
            copies.append(pltpu.make_async_copy(source, target, sem.at[i * PIECES + j]))
            copies[-1].start()
    return copies


def finished(copies):
    for copy in copies:
        copy.wait()


def stage_kernel(filt_hbm, weight_hbm, fwd_ref, bwd_ref, pair0_ref, pair1_ref,
                 filt_ref, filt_sem, sem0, sem1):
    load = pltpu.make_async_copy(filt_hbm, filt_ref, filt_sem)
    load.start()
    copies = fetched(weight_hbm, pair0_ref, sem0, 0)
    copies += fetched(weight_hbm, pair1_ref, sem1, 1)
    load.wait()
    groups, taps = filt_ref.shape
    filt = filt_ref[...]
    flipped = dot(filt, reversal(taps))
    filt = filt.astype(F32)
    zeros = jnp.zeros((1, taps), F32)
    for g in range(groups):
        for source, out_ref, first in ((flipped, fwd_ref, 1), (filt, bwd_ref, 0)):
            row = jnp.concatenate([source[g : g + 1], zeros], axis=1)
            full = jnp.broadcast_to(row, (taps, 2 * taps))
            out_ref[g] = pltpu.roll(
                full, first, axis=1, stride=1, stride_axis=0
            ).astype(BF16)
    finished(copies)


def forward_kernel(group_size, before_ref, inner_ref, query_ref, skip_ref, fwd_ref,
                   ring1_ref, ring2_ref, weight_hbm,
                   mixed_ref, gated_ref, flipped_ref, packed_ref, pair_ref, sem):
    copies = fetched(weight_hbm, pair_ref, sem, 2)
    packed_ref[0] = ring1_ref[...]
    packed_ref[1] = ring2_ref[...]
    rows = inner_ref.shape[0]
    inner = inner_ref[...]
    series = jnp.concatenate([before_ref[...], inner], axis=0)
    mixed = grouped_conv(fwd_ref, series, group_size)
    mixed = mixed + skip_ref[...] * inner.astype(F32)
    mixed_ref[...] = mixed
    gated_ref[...] = (query_ref[...].astype(F32) * mixed).astype(BF16)
    flipped_ref[:rows - 16] = jnp.zeros((rows - 16, inner.shape[1]), BF16)
    flipped_ref[rows - 16 :] = dot(reversal(2 * rows), series).astype(BF16)
    finished(copies)


def products(blocks, pair_ref):
    total = None
    for i, block in enumerate(blocks):
        term = lax.dot_general(block, pair_ref[i], NT, preferred_element_type=F32)
        total = term if total is None else total + term
    return total


def first_product_kernel(own_ref, swap_ref, pair_ref, out_ref):
    out_ref[...] = products((own_ref[...], swap_ref[...]), pair_ref)


def second_product_kernel(ring1_ref, ring2_ref, pair_ref, acc_ref, weight_hbm,
                          out_ref, next_ref, sem):
    copies = fetched(weight_hbm, next_ref, sem, 3)
    out_ref[...] = acc_ref[...] + products((ring1_ref[...], ring2_ref[...]), pair_ref)
    finished(copies)


def third_product_kernel(swaps_ref, pair_ref, acc_ref, out_ref):
    out_ref[...] = acc_ref[...] + products((swaps_ref[0], swaps_ref[1]), pair_ref)


def gradient_kernel(group_size, pair_ref, first_ref, second_ref, acc_ref,
                    query_ref, mixed_ref, inner_ref, flipped_ref,
                    conv_ref, qgrad_ref, sums_ref):
    rows, width = acc_ref.shape
    mixed_grad = acc_ref[...] + products((first_ref[...], second_ref[...]), pair_ref)
    conv = (mixed_grad * query_ref[...].astype(F32)).astype(BF16)
    conv_ref[...] = conv
    qgrad_ref[...] = (mixed_grad * mixed_ref[...]).astype(BF16)
    skip = jnp.sum(conv.astype(F32) * inner_ref[...].astype(F32), axis=0, keepdims=True)
    per_tile = LANES // group_size
    span = 2 * rows
    sub = 16
    row_group = lax.broadcasted_iota(jnp.int32, (per_tile * sub, LANES), 0) // sub
    lane_group = lax.broadcasted_iota(jnp.int32, (per_tile * sub, LANES), 1) // group_size
    own = row_group == lane_group
    found = []
    for tile in range(width // LANES):
        lanes = slice(tile * LANES, (tile + 1) * LANES)
        total = None
        for a in range(rows // sub):
            part = conv[a * sub : (a + 1) * sub, lanes]
            spread = jnp.concatenate([part] * per_tile, axis=0)
            spread = jnp.where(own, spread, jnp.zeros_like(spread))
            start = rows - sub - a * sub
            term = lax.dot_general(
                spread, flipped_ref[start : start + span, lanes], NT,
                preferred_element_type=F32,
            )
            total = term if total is None else total + term
        for g in range(per_tile):
            skewed = pltpu.roll(
                total[g * sub : (g + 1) * sub], 1, axis=1, stride=1, stride_axis=0
            )
            found.append(jnp.sum(skewed[:, rows:], axis=0, keepdims=True))
    found += [skip[:, i * LANES : (i + 1) * LANES] for i in range(width // LANES)]
    found.append(jnp.zeros((sums_ref.shape[1] - len(found), LANES), F32))
    sums = jnp.concatenate(found, axis=0)
    for i in range(sums_ref.shape[0]):
        sums_ref[i] = sums


def fold_kernel(got_ref, out_ref):
    total = jnp.sum(got_ref[...], axis=0)
    for i in range(out_ref.shape[0]):
        out_ref[i] = total


def finish_kernel(got_ref, filter_ref, skip_ref):
    total = jnp.sum(got_ref[...], axis=0)
    groups = filter_ref.shape[0]
    filter_ref[...] = total[:groups]
    for i in range(skip_ref.shape[1] // LANES):
        skip_ref[:, i * LANES : (i + 1) * LANES] = total[groups + i : groups + i + 1]


def backward_kernel(group_size, conv_ref, after_ref, key_ref, value_ref, skip_ref, bwd_ref,
                    kgrad_ref, vgrad_ref):
    conv = conv_ref[...]
    series = jnp.concatenate([conv, after_ref[...]], axis=0)
    grad = grouped_conv(bwd_ref, series, group_size)
    grad = grad + skip_ref[...] * conv.astype(F32)
    kgrad_ref[...] = (grad * value_ref[...].astype(F32)).astype(BF16)
    vgrad_ref[...] = (grad * key_ref[...].astype(F32)).astype(BF16)


def call(kernel, outs, args, flops, specs=None, scratch=(), vmem=24):
    return pl.pallas_call(
        kernel,
        out_shape=[jax.ShapeDtypeStruct(s, d) for s, d in outs],
        in_specs=specs or [VMEM_SPEC] * len(args),
        out_specs=[VMEM_SPEC] * len(outs),
        scratch_shapes=scratch,
        compiler_params=pltpu.CompilerParams(vmem_limit_bytes=vmem << 20),
        cost_estimate=cost(flops, 4 << 20),
    )(*args)


def passed_along(block, axis, distance):
    devices = range(lax.axis_size(axis))
    route = [(i - distance, i) for i in devices if i - distance in devices]
    return lax.ppermute(block, axis, route)


def exchanged(blocks, groups):
    return lax.all_to_all(blocks, "ctx", 0, 0, axis_index_groups=groups, tiled=True)


def per_device(query_act, key_act, value_act, filters, skip_bias, out_weight, out_grad):
    rows, width = query_act.shape
    groups, taps = filters.shape
    group_size = width // groups
    depth = out_grad.shape[1]
    ch_size = lax.axis_size("ch")
    ctx_size = lax.axis_size("ctx")
    chips = ch_size // CORES

    def ring(block):
        to = lambda c: ((c // CORES + (1 if c % CORES == 0 else -1)) % chips) * CORES + c % CORES
        return lax.ppermute(block, "ch", [(c, to(c)) for c in range(ch_size)])

    def swap(block):
        return lax.ppermute(block, "ch", [(c, c ^ 1) for c in range(ch_size)])

    skip_row = skip_bias.reshape(1, width)
    inner = (key_act.astype(F32) * value_act.astype(F32)).astype(BF16)

    hbm = pl.BlockSpec(memory_space=pltpu.HBM)
    pair = ((2, width, depth), BF16)
    wide = (rows, width)
    sem = [pltpu.SemaphoreType.DMA((2 * PIECES,))]

    ring1 = ring(out_grad)
    swap0 = swap(out_grad)
    before = passed_along(inner, "ctx", 1)
    ring2 = ring(swap0)
    fwd, bwd, pair0, pair1 = call(
        stage_kernel,
        [((groups, taps, 2 * taps), BF16)] * 2 + [pair] * 2,
        (filters, out_weight),
        8 * groups * taps * taps,
        [hbm, hbm],
        [pltpu.VMEM(filters.shape, BF16), pltpu.SemaphoreType.DMA] + sem * 2,
        VMEM_MIB,
    )
    acc = call(
        first_product_kernel,
        [(wide, F32)],
        (out_grad, swap0, pair0),
        4 * rows * depth * width,
    )[0]
    ring3 = ring(ring1)
    mixed, gated, flipped, packed, pair2 = call(
        functools.partial(forward_kernel, group_size),
        [(wide, F32), (wide, BF16), ((3 * rows - 16, width), BF16), ((2, rows, depth), BF16), pair],
        (before, inner, query_act, skip_row, fwd, ring1, ring2, out_weight),
        4 * rows * rows * width * 8,
        [VMEM_SPEC] * 7 + [hbm],
        sem,
        VMEM_MIB,
    )
    swap12 = swap(packed)
    acc, pair3 = call(
        second_product_kernel,
        [(wide, F32), pair],
        (ring1, ring2, pair1, acc, out_weight),
        4 * rows * depth * width,
        [VMEM_SPEC] * 4 + [hbm],
        sem,
        VMEM_MIB,
    )
    swap3 = swap(ring3)
    acc = call(
        third_product_kernel,
        [(wide, F32)],
        (swap12, pair2, acc),
        4 * rows * depth * width,
    )[0]
    planes = ctx_size // Z_SIZE
    conv, query_grad, sums = call(
        functools.partial(gradient_kernel, group_size),
        [(wide, BF16), (wide, BF16), ((Z_SIZE, SUM_ROWS, LANES), F32)],
        (pair3, ring3, swap3, acc, query_act, mixed, inner, flipped),
        8 * rows * depth * width,
    )
    along_z = [[p * Z_SIZE + z for z in range(Z_SIZE)] for p in range(planes)]
    across_z = [[p * Z_SIZE + z for p in range(planes)] for z in range(Z_SIZE)]
    sums = exchanged(sums, along_z)
    after = passed_along(conv, "ctx", -1)
    sums = call(fold_kernel, [((planes, SUM_ROWS, LANES), F32)], (sums,), 1 << 20)[0]
    sums = exchanged(sums, across_z)
    key_grad, value_grad = call(
        functools.partial(backward_kernel, group_size),
        [(wide, BF16)] * 2,
        (conv, after, key_act, value_act, skip_row, bwd),
        4 * rows * rows * width * 8,
    )
    filter_grad, skip_grad = call(
        finish_kernel, [((groups, LANES), F32), ((1, width), F32)], (sums,), 1 << 20
    )
    return gated, query_grad, key_grad, value_grad, filter_grad, skip_grad.reshape(width)


def solution(mesh):
    wide, narrow = P("ctx", "ch"), P("ch", None)

    return jax.shard_map(
        per_device,
        mesh=mesh,
        in_specs=(wide, wide, wide, narrow, P("ch"), narrow, wide),
        out_specs=(wide, wide, wide, wide, narrow, P("ch")),
        check_vma=False,
    )
```

```python
import functools

import jax
import jax.numpy as jnp
from jax import lax
from jax.experimental import pallas as pl
from jax.experimental.pallas import tpu as pltpu
from jax.sharding import PartitionSpec as P


BF16 = jnp.bfloat16
F32 = jnp.float32
LANES = 128
Z_SIZE = 8
CORES = 2
SUM_ROWS = 40
VMEM_MIB = 42
PAIR_DISTANCE = (0, -1, 1, 2)
SWAPPED_PAIR = 2

VMEM_SPEC = pl.BlockSpec(memory_space=pltpu.VMEM)
NT = (((1,), (1,)), ((), ()))


def dot(a, b):
    return jnp.dot(a, b, preferred_element_type=F32)


def cost(flops, nbytes):
    return pl.CostEstimate(flops=flops, bytes_accessed=nbytes, transcendentals=0)


def group_mask(rows, group, group_size):
    lane = lax.broadcasted_iota(jnp.int32, (rows, LANES), 1)
    return (lane // group_size) == group


def reversal(size):
    row = lax.broadcasted_iota(jnp.int32, (size, size), 0)
    col = lax.broadcasted_iota(jnp.int32, (size, size), 1)
    return (row + col == size - 1).astype(BF16)


def grouped_conv(table_ref, series, group_size):
    tiles = []
    per_tile = LANES // group_size
    for tile in range(series.shape[1] // LANES):
        block = series[:, tile * LANES : (tile + 1) * LANES]
        total = None
        for g in range(per_tile):
            mask = group_mask(block.shape[0], g, group_size)
            part = jnp.where(mask, block, jnp.zeros_like(block))
            term = dot(table_ref[tile * per_tile + g], part)
            total = term if total is None else total + term
        tiles.append(total)
    return jnp.concatenate(tiles, axis=1)


def positions(pair):
    size = lax.axis_size("ch")
    me = lax.axis_index("ch")
    chips = size // CORES
    chip, core = me // CORES, me % CORES
    step = 1 - 2 * core
    owner = (chip + PAIR_DISTANCE[pair] * step + chips) % chips
    first = 1 - core if pair == SWAPPED_PAIR else core
    return [owner * CORES + first, owner * CORES + 1 - first]


def load_kernel(weight_hbm, blocks_ref, sem):
    depth = blocks_ref.shape[2]
    copies = []
    for pair in range(len(PAIR_DISTANCE)):
        for i, position in enumerate(positions(pair)):
            columns = pl.ds(pl.multiple_of(position * depth, depth), depth)
            slot = 2 * pair + i
            copies.append(
                pltpu.make_async_copy(
                    weight_hbm.at[:, columns], blocks_ref.at[slot], sem.at[slot]
                )
            )
            copies[-1].start()
    for copy in copies:
        copy.wait()


def tables_kernel(filt_ref, fwd_ref, bwd_ref):
    groups, taps = filt_ref.shape
    filt = filt_ref[...]
    flipped = dot(filt, reversal(taps))
    filt = filt.astype(F32)
    zeros = jnp.zeros((1, taps), F32)
    for g in range(groups):
        for source, out_ref, first in ((flipped, fwd_ref, 1), (filt, bwd_ref, 0)):
            row = jnp.concatenate([source[g : g + 1], zeros], axis=1)
            full = jnp.broadcast_to(row, (taps, 2 * taps))
            out_ref[g] = pltpu.roll(
                full, first, axis=1, stride=1, stride_axis=0
            ).astype(BF16)


def forward_kernel(group_size, before_ref, inner_ref, query_ref, skip_ref, fwd_ref,
                   ring1_ref, ring2_ref, mixed_ref, gated_ref, flipped_ref, packed_ref):
    packed_ref[0] = ring1_ref[...]
    packed_ref[1] = ring2_ref[...]
    rows = inner_ref.shape[0]
    inner = inner_ref[...]
    series = jnp.concatenate([before_ref[...], inner], axis=0)
    mixed = grouped_conv(fwd_ref, series, group_size)
    mixed = mixed + skip_ref[...] * inner.astype(F32)
    mixed_ref[...] = mixed
    gated_ref[...] = (query_ref[...].astype(F32) * mixed).astype(BF16)
    flipped_ref[:rows - 16] = jnp.zeros((rows - 16, inner.shape[1]), BF16)
    flipped_ref[rows - 16 :] = dot(reversal(2 * rows), series).astype(BF16)


def products(received, blocks_ref, pair):
    total = None
    for i, block in enumerate(received):
        weight = blocks_ref[2 * pair + i]
        term = lax.dot_general(block, weight, NT, preferred_element_type=F32)
        total = term if total is None else total + term
    return total


def first_product_kernel(own_ref, swap_ref, blocks_ref, out_ref):
    out_ref[...] = products((own_ref[...], swap_ref[...]), blocks_ref, 0)


def second_product_kernel(ring1_ref, ring2_ref, blocks_ref, acc_ref, out_ref):
    out_ref[...] = acc_ref[...] + products((ring1_ref[...], ring2_ref[...]), blocks_ref, 1)


def third_product_kernel(swaps_ref, blocks_ref, acc_ref, out_ref):
    out_ref[...] = acc_ref[...] + products((swaps_ref[0], swaps_ref[1]), blocks_ref, 2)


def gradient_kernel(group_size, blocks_ref, first_ref, second_ref, acc_ref,
                    query_ref, mixed_ref, inner_ref, flipped_ref,
                    conv_ref, qgrad_ref, sums_ref):
    rows, width = acc_ref.shape
    mixed_grad = acc_ref[...] + products((first_ref[...], second_ref[...]), blocks_ref, 3)
    conv = (mixed_grad * query_ref[...].astype(F32)).astype(BF16)
    conv_ref[...] = conv
    qgrad_ref[...] = (mixed_grad * mixed_ref[...]).astype(BF16)
    skip = jnp.sum(conv.astype(F32) * inner_ref[...].astype(F32), axis=0, keepdims=True)
    per_tile = LANES // group_size
    span = 2 * rows
    sub = 16
    row_group = lax.broadcasted_iota(jnp.int32, (per_tile * sub, LANES), 0) // sub
    lane_group = lax.broadcasted_iota(jnp.int32, (per_tile * sub, LANES), 1) // group_size
    own = row_group == lane_group
    found = []
    for tile in range(width // LANES):
        lanes = slice(tile * LANES, (tile + 1) * LANES)
        total = None
        for a in range(rows // sub):
            part = conv[a * sub : (a + 1) * sub, lanes]
            spread = jnp.concatenate([part] * per_tile, axis=0)
            spread = jnp.where(own, spread, jnp.zeros_like(spread))
            start = rows - sub - a * sub
            term = lax.dot_general(
                spread, flipped_ref[start : start + span, lanes], NT,
                preferred_element_type=F32,
            )
            total = term if total is None else total + term
        for g in range(per_tile):
            skewed = pltpu.roll(
                total[g * sub : (g + 1) * sub], 1, axis=1, stride=1, stride_axis=0
            )
            found.append(jnp.sum(skewed[:, rows:], axis=0, keepdims=True))
    found += [skip[:, i * LANES : (i + 1) * LANES] for i in range(width // LANES)]
    found.append(jnp.zeros((sums_ref.shape[1] - len(found), LANES), F32))
    sums = jnp.concatenate(found, axis=0)
    for i in range(sums_ref.shape[0]):
        sums_ref[i] = sums


def fold_kernel(got_ref, out_ref):
    total = jnp.sum(got_ref[...], axis=0)
    for i in range(out_ref.shape[0]):
        out_ref[i] = total


def finish_kernel(got_ref, filter_ref, skip_ref):
    total = jnp.sum(got_ref[...], axis=0)
    groups = filter_ref.shape[0]
    filter_ref[...] = total[:groups]
    for i in range(skip_ref.shape[1] // LANES):
        skip_ref[:, i * LANES : (i + 1) * LANES] = total[groups + i : groups + i + 1]


def backward_kernel(group_size, conv_ref, after_ref, key_ref, value_ref, skip_ref, bwd_ref,
                    kgrad_ref, vgrad_ref):
    conv = conv_ref[...]
    series = jnp.concatenate([conv, after_ref[...]], axis=0)
    grad = grouped_conv(bwd_ref, series, group_size)
    grad = grad + skip_ref[...] * conv.astype(F32)
    kgrad_ref[...] = (grad * value_ref[...].astype(F32)).astype(BF16)
    vgrad_ref[...] = (grad * key_ref[...].astype(F32)).astype(BF16)


def call(kernel, outs, args, flops, specs=None, scratch=(), vmem=24):
    return pl.pallas_call(
        kernel,
        out_shape=[jax.ShapeDtypeStruct(s, d) for s, d in outs],
        in_specs=specs or [VMEM_SPEC] * len(args),
        out_specs=[VMEM_SPEC] * len(outs),
        scratch_shapes=scratch,
        compiler_params=pltpu.CompilerParams(vmem_limit_bytes=vmem << 20),
        cost_estimate=cost(flops, 4 << 20),
    )(*args)


def passed_along(block, axis, distance):
    devices = range(lax.axis_size(axis))
    route = [(i - distance, i) for i in devices if i - distance in devices]
    return lax.ppermute(block, axis, route)


def exchanged(blocks, groups):
    return lax.all_to_all(blocks, "ctx", 0, 0, axis_index_groups=groups, tiled=True)


def per_device(query_act, key_act, value_act, filters, skip_bias, out_weight, out_grad):
    rows, width = query_act.shape
    groups, taps = filters.shape
    group_size = width // groups
    depth = out_grad.shape[1]
    ch_size = lax.axis_size("ch")
    ctx_size = lax.axis_size("ctx")
    chips = ch_size // CORES

    def ring(block):
        to = lambda c: ((c // CORES + (1 if c % CORES == 0 else -1)) % chips) * CORES + c % CORES
        return lax.ppermute(block, "ch", [(c, to(c)) for c in range(ch_size)])

    def swap(block):
        return lax.ppermute(block, "ch", [(c, c ^ 1) for c in range(ch_size)])

    skip_row = skip_bias.reshape(1, width)
    inner = (key_act.astype(F32) * value_act.astype(F32)).astype(BF16)

    hbm = pl.BlockSpec(memory_space=pltpu.HBM)
    wide = (rows, width)

    ring1 = ring(out_grad)
    swap0 = swap(out_grad)
    before = passed_along(inner, "ctx", 1)
    ring2 = ring(swap0)
    blocks = call(
        load_kernel,
        [((ch_size, width, depth), BF16)],
        (out_weight,),
        1 << 20,
        [hbm],
        [pltpu.SemaphoreType.DMA((ch_size,))],
        VMEM_MIB,
    )[0]
    ring3 = ring(ring1)
    fwd, bwd = call(
        tables_kernel, [((groups, taps, 2 * taps), BF16)] * 2, (filters,), 8 * groups * taps * taps
    )
    mixed, gated, flipped, packed = call(
        functools.partial(forward_kernel, group_size),
        [(wide, F32), (wide, BF16), ((3 * rows - 16, width), BF16), ((2, rows, depth), BF16)],
        (before, inner, query_act, skip_row, fwd, ring1, ring2),
        4 * rows * rows * width * 8,
    )
    swap12 = swap(packed)
    acc = call(
        first_product_kernel, [(wide, F32)], (out_grad, swap0, blocks), 4 * rows * depth * width
    )[0]
    acc = call(
        second_product_kernel, [(wide, F32)], (ring1, ring2, blocks, acc), 4 * rows * depth * width
    )[0]
    swap3 = swap(ring3)
    acc = call(
        third_product_kernel, [(wide, F32)], (swap12, blocks, acc), 4 * rows * depth * width
    )[0]
    planes = ctx_size // Z_SIZE
    conv, query_grad, sums = call(
        functools.partial(gradient_kernel, group_size),
        [(wide, BF16), (wide, BF16), ((Z_SIZE, SUM_ROWS, LANES), F32)],
        (blocks, ring3, swap3, acc, query_act, mixed, inner, flipped),
        8 * rows * depth * width,
    )
    along_z = [[p * Z_SIZE + z for z in range(Z_SIZE)] for p in range(planes)]
    across_z = [[p * Z_SIZE + z for p in range(planes)] for z in range(Z_SIZE)]
    sums = exchanged(sums, along_z)
    after = passed_along(conv, "ctx", -1)
    sums = call(fold_kernel, [((planes, SUM_ROWS, LANES), F32)], (sums,), 1 << 20)[0]
    sums = exchanged(sums, across_z)
    key_grad, value_grad = call(
        functools.partial(backward_kernel, group_size),
        [(wide, BF16)] * 2,
        (conv, after, key_act, value_act, skip_row, bwd),
        4 * rows * rows * width * 8,
    )
    filter_grad, skip_grad = call(
        finish_kernel, [((groups, LANES), F32), ((1, width), F32)], (sums,), 1 << 20
    )
    return gated, query_grad, key_grad, value_grad, filter_grad, skip_grad.reshape(width)


def solution(mesh):
    wide, narrow = P("ctx", "ch"), P("ch", None)

    return jax.shard_map(
        per_device,
        mesh=mesh,
        in_specs=(wide, wide, wide, narrow, P("ch"), narrow, wide),
        out_specs=(wide, wide, wide, wide, narrow, P("ch")),
        check_vma=False,
    )
```

```python
import functools

import jax
import jax.numpy as jnp
from jax import lax
from jax.experimental import pallas as pl
from jax.experimental.pallas import tpu as pltpu
from jax.sharding import PartitionSpec as P


BF16 = jnp.bfloat16
F32 = jnp.float32
LANES = 128
X_SIZE = 8
CORES = 2
SUM_ROWS = 40
VMEM_MIB = 42
PAIR_DISTANCE = (0, -1, 1, 2)
SWAPPED_PAIR = 2

VMEM_SPEC = pl.BlockSpec(memory_space=pltpu.VMEM)
NT = (((1,), (1,)), ((), ()))


def dot(a, b):
    return jnp.dot(a, b, preferred_element_type=F32)


def cost(flops, nbytes):
    return pl.CostEstimate(flops=flops, bytes_accessed=nbytes, transcendentals=0)


def group_mask(rows, group, group_size):
    lane = lax.broadcasted_iota(jnp.int32, (rows, LANES), 1)
    return (lane // group_size) == group


def reversal(size):
    row = lax.broadcasted_iota(jnp.int32, (size, size), 0)
    col = lax.broadcasted_iota(jnp.int32, (size, size), 1)
    return (row + col == size - 1).astype(BF16)


def grouped_conv(table_ref, series, group_size):
    tiles = []
    per_tile = LANES // group_size
    for tile in range(series.shape[1] // LANES):
        block = series[:, tile * LANES : (tile + 1) * LANES]
        total = None
        for g in range(per_tile):
            mask = group_mask(block.shape[0], g, group_size)
            part = jnp.where(mask, block, jnp.zeros_like(block))
            term = dot(table_ref[tile * per_tile + g], part)
            total = term if total is None else total + term
        tiles.append(total)
    return jnp.concatenate(tiles, axis=1)


def positions(pair):
    size = lax.axis_size("ch")
    me = lax.axis_index("ch")
    chips = size // CORES
    chip, core = me // CORES, me % CORES
    step = 1 - 2 * core
    owner = (chip + PAIR_DISTANCE[pair] * step + chips) % chips
    first = 1 - core if pair == SWAPPED_PAIR else core
    return [owner * CORES + first, owner * CORES + 1 - first]


def load_kernel(weight_hbm, blocks_ref, sem):
    depth = blocks_ref.shape[2]
    copies = []
    for pair in range(len(PAIR_DISTANCE)):
        for i, position in enumerate(positions(pair)):
            columns = pl.ds(pl.multiple_of(position * depth, depth), depth)
            slot = 2 * pair + i
            copies.append(
                pltpu.make_async_copy(
                    weight_hbm.at[:, columns], blocks_ref.at[slot], sem.at[slot]
                )
            )
            copies[-1].start()
    for copy in copies:
        copy.wait()


def tables_kernel(filt_ref, fwd_ref, bwd_ref):
    groups, taps = filt_ref.shape
    filt = filt_ref[...]
    flipped = dot(filt, reversal(taps))
    filt = filt.astype(F32)
    zeros = jnp.zeros((1, taps), F32)
    for g in range(groups):
        for source, out_ref, first in ((flipped, fwd_ref, 1), (filt, bwd_ref, 0)):
            row = jnp.concatenate([source[g : g + 1], zeros], axis=1)
            full = jnp.broadcast_to(row, (taps, 2 * taps))
            out_ref[g] = pltpu.roll(
                full, first, axis=1, stride=1, stride_axis=0
            ).astype(BF16)


def forward_kernel(group_size, before_ref, inner_ref, query_ref, skip_ref, fwd_ref,
                   ring1_ref, ring2_ref, mixed_ref, gated_ref, flipped_ref, packed_ref):
    packed_ref[0] = ring1_ref[...]
    packed_ref[1] = ring2_ref[...]
    rows = inner_ref.shape[0]
    inner = inner_ref[...]
    series = jnp.concatenate([before_ref[...], inner], axis=0)
    mixed = grouped_conv(fwd_ref, series, group_size)
    mixed = mixed + skip_ref[...] * inner.astype(F32)
    mixed_ref[...] = mixed
    gated_ref[...] = (query_ref[...].astype(F32) * mixed).astype(BF16)
    flipped_ref[:rows - 16] = jnp.zeros((rows - 16, inner.shape[1]), BF16)
    flipped_ref[rows - 16 :] = dot(reversal(2 * rows), series).astype(BF16)


def products(received, blocks_ref, pair):
    total = None
    for i, block in enumerate(received):
        weight = blocks_ref[2 * pair + i]
        term = lax.dot_general(block, weight, NT, preferred_element_type=F32)
        total = term if total is None else total + term
    return total


def first_product_kernel(own_ref, swap_ref, blocks_ref, out_ref):
    out_ref[...] = products((own_ref[...], swap_ref[...]), blocks_ref, 0)


def second_product_kernel(ring1_ref, ring2_ref, blocks_ref, acc_ref, out_ref):
    out_ref[...] = acc_ref[...] + products((ring1_ref[...], ring2_ref[...]), blocks_ref, 1)


def third_product_kernel(swaps_ref, blocks_ref, acc_ref, out_ref):
    out_ref[...] = acc_ref[...] + products((swaps_ref[0], swaps_ref[1]), blocks_ref, 2)


def gradient_kernel(group_size, blocks_ref, first_ref, second_ref, acc_ref,
                    query_ref, mixed_ref, inner_ref, flipped_ref,
                    conv_ref, qgrad_ref, sums_ref):
    rows, width = acc_ref.shape
    mixed_grad = acc_ref[...] + products((first_ref[...], second_ref[...]), blocks_ref, 3)
    conv = (mixed_grad * query_ref[...].astype(F32)).astype(BF16)
    conv_ref[...] = conv
    qgrad_ref[...] = (mixed_grad * mixed_ref[...]).astype(BF16)
    skip = jnp.sum(conv.astype(F32) * inner_ref[...].astype(F32), axis=0, keepdims=True)
    per_tile = LANES // group_size
    span = 2 * rows
    sub = 16
    row_group = lax.broadcasted_iota(jnp.int32, (per_tile * sub, LANES), 0) // sub
    lane_group = lax.broadcasted_iota(jnp.int32, (per_tile * sub, LANES), 1) // group_size
    own = row_group == lane_group
    found = []
    for tile in range(width // LANES):
        lanes = slice(tile * LANES, (tile + 1) * LANES)
        total = None
        for a in range(rows // sub):
            part = conv[a * sub : (a + 1) * sub, lanes]
            spread = jnp.concatenate([part] * per_tile, axis=0)
            spread = jnp.where(own, spread, jnp.zeros_like(spread))
            start = rows - sub - a * sub
            term = lax.dot_general(
                spread, flipped_ref[start : start + span, lanes], NT,
                preferred_element_type=F32,
            )
            total = term if total is None else total + term
        for g in range(per_tile):
            skewed = pltpu.roll(
                total[g * sub : (g + 1) * sub], 1, axis=1, stride=1, stride_axis=0
            )
            found.append(jnp.sum(skewed[:, rows:], axis=0, keepdims=True))
    found += [skip[:, i * LANES : (i + 1) * LANES] for i in range(width // LANES)]
    found.append(jnp.zeros((sums_ref.shape[1] - len(found), LANES), F32))
    sums = jnp.concatenate(found, axis=0)
    for i in range(sums_ref.shape[0]):
        sums_ref[i] = sums


def fold_kernel(got_ref, out_ref):
    total = jnp.sum(got_ref[...], axis=0)
    for i in range(out_ref.shape[0]):
        out_ref[i] = total


def finish_kernel(got_ref, filter_ref, skip_ref):
    total = jnp.sum(got_ref[...], axis=0)
    groups = filter_ref.shape[0]
    filter_ref[...] = total[:groups]
    for i in range(skip_ref.shape[1] // LANES):
        skip_ref[:, i * LANES : (i + 1) * LANES] = total[groups + i : groups + i + 1]


def backward_kernel(group_size, conv_ref, after_ref, key_ref, value_ref, skip_ref, bwd_ref,
                    kgrad_ref, vgrad_ref):
    conv = conv_ref[...]
    series = jnp.concatenate([conv, after_ref[...]], axis=0)
    grad = grouped_conv(bwd_ref, series, group_size)
    grad = grad + skip_ref[...] * conv.astype(F32)
    kgrad_ref[...] = (grad * value_ref[...].astype(F32)).astype(BF16)
    vgrad_ref[...] = (grad * key_ref[...].astype(F32)).astype(BF16)


def call(kernel, outs, args, flops, specs=None, scratch=(), vmem=24):
    return pl.pallas_call(
        kernel,
        out_shape=[jax.ShapeDtypeStruct(s, d) for s, d in outs],
        in_specs=specs or [VMEM_SPEC] * len(args),
        out_specs=[VMEM_SPEC] * len(outs),
        scratch_shapes=scratch,
        compiler_params=pltpu.CompilerParams(vmem_limit_bytes=vmem << 20),
        cost_estimate=cost(flops, 4 << 20),
    )(*args)


def passed_along(block, axis, distance):
    devices = range(lax.axis_size(axis))
    route = [(i - distance, i) for i in devices if i - distance in devices]
    return lax.ppermute(block, axis, route)


def exchanged(blocks, groups):
    return lax.all_to_all(blocks, "ctx", 0, 0, axis_index_groups=groups, tiled=True)


def per_device(query_act, key_act, value_act, filters, skip_bias, out_weight, out_grad):
    rows, width = query_act.shape
    groups, taps = filters.shape
    group_size = width // groups
    depth = out_grad.shape[1]
    ch_size = lax.axis_size("ch")
    ctx_size = lax.axis_size("ctx")
    chips = ch_size // CORES

    def ring(block):
        to = lambda c: ((c // CORES + (1 if c % CORES == 0 else -1)) % chips) * CORES + c % CORES
        return lax.ppermute(block, "ch", [(c, to(c)) for c in range(ch_size)])

    def swap(block):
        return lax.ppermute(block, "ch", [(c, c ^ 1) for c in range(ch_size)])

    skip_row = skip_bias.reshape(1, width)
    inner = (key_act.astype(F32) * value_act.astype(F32)).astype(BF16)

    hbm = pl.BlockSpec(memory_space=pltpu.HBM)
    wide = (rows, width)

    ring1 = ring(out_grad)
    swap0 = swap(out_grad)
    before = passed_along(inner, "ctx", 1)
    ring2 = ring(swap0)
    blocks = call(
        load_kernel,
        [((ch_size, width, depth), BF16)],
        (out_weight,),
        1 << 20,
        [hbm],
        [pltpu.SemaphoreType.DMA((ch_size,))],
        VMEM_MIB,
    )[0]
    ring3 = ring(ring1)
    fwd, bwd = call(
        tables_kernel, [((groups, taps, 2 * taps), BF16)] * 2, (filters,), 8 * groups * taps * taps
    )
    mixed, gated, flipped, packed = call(
        functools.partial(forward_kernel, group_size),
        [(wide, F32), (wide, BF16), ((3 * rows - 16, width), BF16), ((2, rows, depth), BF16)],
        (before, inner, query_act, skip_row, fwd, ring1, ring2),
        4 * rows * rows * width * 8,
    )
    swap12 = swap(packed)
    acc = call(
        first_product_kernel, [(wide, F32)], (out_grad, swap0, blocks), 4 * rows * depth * width
    )[0]
    acc = call(
        second_product_kernel, [(wide, F32)], (ring1, ring2, blocks, acc), 4 * rows * depth * width
    )[0]
    swap3 = swap(ring3)
    acc = call(
        third_product_kernel, [(wide, F32)], (swap12, blocks, acc), 4 * rows * depth * width
    )[0]
    near = ctx_size // X_SIZE
    conv, query_grad, sums = call(
        functools.partial(gradient_kernel, group_size),
        [(wide, BF16), (wide, BF16), ((X_SIZE, SUM_ROWS, LANES), F32)],
        (blocks, ring3, swap3, acc, query_act, mixed, inner, flipped),
        8 * rows * depth * width,
    )
    along_x = [[x * near + r for x in range(X_SIZE)] for r in range(near)]
    same_x = [[x * near + r for r in range(near)] for x in range(X_SIZE)]
    sums = exchanged(sums, along_x)
    after = passed_along(conv, "ctx", -1)
    sums = call(fold_kernel, [((near, SUM_ROWS, LANES), F32)], (sums,), 1 << 20)[0]
    sums = exchanged(sums, same_x)
    key_grad, value_grad = call(
        functools.partial(backward_kernel, group_size),
        [(wide, BF16)] * 2,
        (conv, after, key_act, value_act, skip_row, bwd),
        4 * rows * rows * width * 8,
    )
    filter_grad, skip_grad = call(
        finish_kernel, [((groups, LANES), F32), ((1, width), F32)], (sums,), 1 << 20
    )
    return gated, query_grad, key_grad, value_grad, filter_grad, skip_grad.reshape(width)


def solution(mesh):
    wide, narrow = P("ctx", "ch"), P("ch", None)

    return jax.shard_map(
        per_device,
        mesh=mesh,
        in_specs=(wide, wide, wide, narrow, P("ch"), narrow, wide),
        out_specs=(wide, wide, wide, wide, narrow, P("ch")),
        check_vma=False,
    )
```

```python
import functools

import jax
import jax.numpy as jnp
from jax import lax
from jax.experimental import pallas as pl
from jax.experimental.pallas import tpu as pltpu
from jax.sharding import PartitionSpec as P


BF16 = jnp.bfloat16
F32 = jnp.float32
LANES = 128
Z_SIZE = 8
Y_LOW = 2
CORES = 2
HALF_ROWS = 24
VMEM_MIB = 42
PAIR_DISTANCE = (0, -1, 1, 2)
SWAPPED_PAIR = 2

VMEM_SPEC = pl.BlockSpec(memory_space=pltpu.VMEM)
NT = (((1,), (1,)), ((), ()))


def dot(a, b):
    return jnp.dot(a, b, preferred_element_type=F32)


def cost(flops, nbytes):
    return pl.CostEstimate(flops=flops, bytes_accessed=nbytes, transcendentals=0)


def group_mask(rows, group, group_size):
    lane = lax.broadcasted_iota(jnp.int32, (rows, LANES), 1)
    return (lane // group_size) == group


def reversal(size):
    row = lax.broadcasted_iota(jnp.int32, (size, size), 0)
    col = lax.broadcasted_iota(jnp.int32, (size, size), 1)
    return (row + col == size - 1).astype(BF16)


def grouped_conv(table_ref, series, group_size):
    tiles = []
    per_tile = LANES // group_size
    for tile in range(series.shape[1] // LANES):
        block = series[:, tile * LANES : (tile + 1) * LANES]
        total = None
        for g in range(per_tile):
            mask = group_mask(block.shape[0], g, group_size)
            part = jnp.where(mask, block, jnp.zeros_like(block))
            term = dot(table_ref[tile * per_tile + g], part)
            total = term if total is None else total + term
        tiles.append(total)
    return jnp.concatenate(tiles, axis=1)


def positions(pair):
    size = lax.axis_size("ch")
    me = lax.axis_index("ch")
    chips = size // CORES
    chip, core = me // CORES, me % CORES
    step = 1 - 2 * core
    owner = (chip + PAIR_DISTANCE[pair] * step + chips) % chips
    first = 1 - core if pair == SWAPPED_PAIR else core
    return [owner * CORES + first, owner * CORES + 1 - first]


def load_kernel(weight_hbm, blocks_ref, sem):
    depth = blocks_ref.shape[2]
    copies = []
    for pair in range(len(PAIR_DISTANCE)):
        for i, position in enumerate(positions(pair)):
            columns = pl.ds(pl.multiple_of(position * depth, depth), depth)
            slot = 2 * pair + i
            copies.append(
                pltpu.make_async_copy(
                    weight_hbm.at[:, columns], blocks_ref.at[slot], sem.at[slot]
                )
            )
            copies[-1].start()
    for copy in copies:
        copy.wait()


def tables_kernel(filt_ref, fwd_ref, bwd_ref):
    groups, taps = filt_ref.shape
    filt = filt_ref[...]
    flipped = dot(filt, reversal(taps))
    filt = filt.astype(F32)
    zeros = jnp.zeros((1, taps), F32)
    for g in range(groups):
        for source, out_ref, first in ((flipped, fwd_ref, 1), (filt, bwd_ref, 0)):
            row = jnp.concatenate([source[g : g + 1], zeros], axis=1)
            full = jnp.broadcast_to(row, (taps, 2 * taps))
            out_ref[g] = pltpu.roll(
                full, first, axis=1, stride=1, stride_axis=0
            ).astype(BF16)


def forward_kernel(group_size, before_ref, inner_ref, query_ref, skip_ref, fwd_ref,
                   ring1_ref, ring2_ref, mixed_ref, gated_ref, flipped_ref, packed_ref):
    packed_ref[0] = ring1_ref[...]
    packed_ref[1] = ring2_ref[...]
    rows = inner_ref.shape[0]
    inner = inner_ref[...]
    series = jnp.concatenate([before_ref[...], inner], axis=0)
    mixed = grouped_conv(fwd_ref, series, group_size)
    mixed = mixed + skip_ref[...] * inner.astype(F32)
    mixed_ref[...] = mixed
    gated_ref[...] = (query_ref[...].astype(F32) * mixed).astype(BF16)
    flipped_ref[:rows - 16] = jnp.zeros((rows - 16, inner.shape[1]), BF16)
    flipped_ref[rows - 16 :] = dot(reversal(2 * rows), series).astype(BF16)


def products(received, blocks_ref, pair):
    total = None
    for i, block in enumerate(received):
        weight = blocks_ref[2 * pair + i]
        term = lax.dot_general(block, weight, NT, preferred_element_type=F32)
        total = term if total is None else total + term
    return total


def first_product_kernel(own_ref, swap_ref, blocks_ref, out_ref):
    out_ref[...] = products((own_ref[...], swap_ref[...]), blocks_ref, 0)


def second_product_kernel(ring1_ref, ring2_ref, blocks_ref, acc_ref, out_ref):
    out_ref[...] = acc_ref[...] + products((ring1_ref[...], ring2_ref[...]), blocks_ref, 1)


def third_product_kernel(swaps_ref, blocks_ref, acc_ref, out_ref):
    out_ref[...] = acc_ref[...] + products((swaps_ref[0], swaps_ref[1]), blocks_ref, 2)


def gradient_kernel(group_size, blocks_ref, first_ref, second_ref, acc_ref,
                    query_ref, mixed_ref, inner_ref, flipped_ref,
                    conv_ref, qgrad_ref, sums_ref):
    rows, width = acc_ref.shape
    mixed_grad = acc_ref[...] + products((first_ref[...], second_ref[...]), blocks_ref, 3)
    conv = (mixed_grad * query_ref[...].astype(F32)).astype(BF16)
    conv_ref[...] = conv
    qgrad_ref[...] = (mixed_grad * mixed_ref[...]).astype(BF16)
    skip = jnp.sum(conv.astype(F32) * inner_ref[...].astype(F32), axis=0, keepdims=True)
    per_tile = LANES // group_size
    span = 2 * rows
    sub = 16
    row_group = lax.broadcasted_iota(jnp.int32, (per_tile * sub, LANES), 0) // sub
    lane_group = lax.broadcasted_iota(jnp.int32, (per_tile * sub, LANES), 1) // group_size
    own = row_group == lane_group
    found = []
    for tile in range(width // LANES):
        lanes = slice(tile * LANES, (tile + 1) * LANES)
        total = None
        for a in range(rows // sub):
            part = conv[a * sub : (a + 1) * sub, lanes]
            spread = jnp.concatenate([part] * per_tile, axis=0)
            spread = jnp.where(own, spread, jnp.zeros_like(spread))
            start = rows - sub - a * sub
            term = lax.dot_general(
                spread, flipped_ref[start : start + span, lanes], NT,
                preferred_element_type=F32,
            )
            total = term if total is None else total + term
        for g in range(per_tile):
            skewed = pltpu.roll(
                total[g * sub : (g + 1) * sub], 1, axis=1, stride=1, stride_axis=0
            )
            found.append(jnp.sum(skewed[:, rows:], axis=0, keepdims=True))
    found_skip = [skip[:, i * LANES : (i + 1) * LANES] for i in range(width // LANES)]
    filt_rows, skip_rows = len(found) // Y_LOW, len(found_skip) // Y_LOW
    zeros = jnp.zeros((HALF_ROWS - filt_rows - skip_rows, LANES), F32)
    halves = []
    for y in range(Y_LOW):
        filt_part = found[y * filt_rows : (y + 1) * filt_rows]
        skip_part = found_skip[y * skip_rows : (y + 1) * skip_rows]
        halves.append(jnp.concatenate(filt_part + skip_part + [zeros], axis=0))
    for i in range(sums_ref.shape[0]):
        sums_ref[i] = halves[i % Y_LOW]


def fold_kernel(got_ref, out_ref):
    total = jnp.sum(got_ref[...], axis=0)
    for i in range(out_ref.shape[0]):
        out_ref[i] = total


def finish_kernel(got_ref, filter_ref, skip_ref):
    along_z = got_ref.shape[0] // Y_LOW
    filt_rows = filter_ref.shape[0] // Y_LOW
    skip_rows = skip_ref.shape[1] // LANES // Y_LOW
    for y in range(Y_LOW):
        total = jnp.sum(got_ref[y * along_z : (y + 1) * along_z], axis=0)
        filter_ref[y * filt_rows : (y + 1) * filt_rows] = total[:filt_rows]
        for i in range(skip_rows):
            at = (y * skip_rows + i) * LANES
            skip_ref[:, at : at + LANES] = total[filt_rows + i : filt_rows + i + 1]


def backward_kernel(group_size, conv_ref, after_ref, key_ref, value_ref, skip_ref, bwd_ref,
                    kgrad_ref, vgrad_ref):
    conv = conv_ref[...]
    series = jnp.concatenate([conv, after_ref[...]], axis=0)
    grad = grouped_conv(bwd_ref, series, group_size)
    grad = grad + skip_ref[...] * conv.astype(F32)
    kgrad_ref[...] = (grad * value_ref[...].astype(F32)).astype(BF16)
    vgrad_ref[...] = (grad * key_ref[...].astype(F32)).astype(BF16)


def call(kernel, outs, args, flops, specs=None, scratch=(), vmem=24):
    return pl.pallas_call(
        kernel,
        out_shape=[jax.ShapeDtypeStruct(s, d) for s, d in outs],
        in_specs=specs or [VMEM_SPEC] * len(args),
        out_specs=[VMEM_SPEC] * len(outs),
        scratch_shapes=scratch,
        compiler_params=pltpu.CompilerParams(vmem_limit_bytes=vmem << 20),
        cost_estimate=cost(flops, 4 << 20),
    )(*args)


def passed_along(block, axis, distance):
    devices = range(lax.axis_size(axis))
    route = [(i - distance, i) for i in devices if i - distance in devices]
    return lax.ppermute(block, axis, route)


def exchanged(blocks, groups):
    return lax.all_to_all(blocks, "ctx", 0, 0, axis_index_groups=groups, tiled=True)


def per_device(query_act, key_act, value_act, filters, skip_bias, out_weight, out_grad):
    rows, width = query_act.shape
    groups, taps = filters.shape
    group_size = width // groups
    depth = out_grad.shape[1]
    ch_size = lax.axis_size("ch")
    ctx_size = lax.axis_size("ctx")
    chips = ch_size // CORES

    def ring(block):
        to = lambda c: ((c // CORES + (1 if c % CORES == 0 else -1)) % chips) * CORES + c % CORES
        return lax.ppermute(block, "ch", [(c, to(c)) for c in range(ch_size)])

    def swap(block):
        return lax.ppermute(block, "ch", [(c, c ^ 1) for c in range(ch_size)])

    skip_row = skip_bias.reshape(1, width)
    inner = (key_act.astype(F32) * value_act.astype(F32)).astype(BF16)

    hbm = pl.BlockSpec(memory_space=pltpu.HBM)
    wide = (rows, width)

    ring1 = ring(out_grad)
    swap0 = swap(out_grad)
    before = passed_along(inner, "ctx", 1)
    ring2 = ring(swap0)
    blocks = call(
        load_kernel,
        [((ch_size, width, depth), BF16)],
        (out_weight,),
        1 << 20,
        [hbm],
        [pltpu.SemaphoreType.DMA((ch_size,))],
        VMEM_MIB,
    )[0]
    ring3 = ring(ring1)
    fwd, bwd = call(
        tables_kernel, [((groups, taps, 2 * taps), BF16)] * 2, (filters,), 8 * groups * taps * taps
    )
    mixed, gated, flipped, packed = call(
        functools.partial(forward_kernel, group_size),
        [(wide, F32), (wide, BF16), ((3 * rows - 16, width), BF16), ((2, rows, depth), BF16)],
        (before, inner, query_act, skip_row, fwd, ring1, ring2),
        4 * rows * rows * width * 8,
    )
    swap12 = swap(packed)
    acc = call(
        first_product_kernel, [(wide, F32)], (out_grad, swap0, blocks), 4 * rows * depth * width
    )[0]
    acc = call(
        second_product_kernel, [(wide, F32)], (ring1, ring2, blocks, acc), 4 * rows * depth * width
    )[0]
    swap3 = swap(ring3)
    acc = call(
        third_product_kernel, [(wide, F32)], (swap12, blocks, acc), 4 * rows * depth * width
    )[0]
    planes, near = ctx_size // Z_SIZE, Y_LOW * Z_SIZE
    conv, query_grad, sums = call(
        functools.partial(gradient_kernel, group_size),
        [(wide, BF16), (wide, BF16), ((planes, HALF_ROWS, LANES), F32)],
        (blocks, ring3, swap3, acc, query_act, mixed, inner, flipped),
        8 * rows * depth * width,
    )
    same_z = [[p * Z_SIZE + z for p in range(planes)] for z in range(Z_SIZE)]
    same_x = [[x * near + r for r in range(near)] for x in range(planes // Y_LOW)]
    sums = exchanged(sums, same_z)
    after = passed_along(conv, "ctx", -1)
    sums = call(fold_kernel, [((near, HALF_ROWS, LANES), F32)], (sums,), 1 << 20)[0]
    sums = exchanged(sums, same_x)
    key_grad, value_grad = call(
        functools.partial(backward_kernel, group_size),
        [(wide, BF16)] * 2,
        (conv, after, key_act, value_act, skip_row, bwd),
        4 * rows * rows * width * 8,
    )
    filter_grad, skip_grad = call(
        finish_kernel, [((groups, LANES), F32), ((1, width), F32)], (sums,), 1 << 20
    )
    return gated, query_grad, key_grad, value_grad, filter_grad, skip_grad.reshape(width)


def solution(mesh):
    wide, narrow = P("ctx", "ch"), P("ch", None)

    return jax.shard_map(
        per_device,
        mesh=mesh,
        in_specs=(wide, wide, wide, narrow, P("ch"), narrow, wide),
        out_specs=(wide, wide, wide, wide, narrow, P("ch")),
        check_vma=False,
    )
```
